32 devices in a mesh: dp: 4 (over y, core), space: 4 (over z), tensor: 2 (over x).
Axes of the slice: x: 2, y: 2, z: 4, core: 2. Of those that a mesh axis runs over, the one named last changes fastest.
Arguments:
- feature_map: bfloat16 [4, 32, 48, 1536], P('dp', 'space', None, 'tensor'), may hold values from -12 to 12
- conv_kernel: float32 [7, 7, 1536], replicated, may hold values from -6 to 6
- conv_bias: float32 [1536], replicated, may hold values from -4 to 4
- norm_gain: float32 [1536], replicated, may hold values from 0.1 to 1.9
- norm_bias: float32 [1536], replicated, may hold values from -3 to 3
- expand_weight: bfloat16 [1536, 6144], P(None, 'tensor'), may hold values from -0.21875 to 0.21875
- expand_bias: float32 [6144], P('tensor'), may hold values from -3 to 3
- project_weight: bfloat16 [6144, 1536], P('tensor'), may hold values from -0.109375 to 0.109375
- project_bias: float32 [1536], P('tensor'), may hold values from -3 to 3
- layer_scale: float32 [1536], P('tensor'), may hold values from 0.3 to 1.5
- cotangent: bfloat16 [4, 32, 48, 1536], P('dp', 'space', None, 'tensor'), may hold values from -6 to 6
Outputs:
- block_out: bfloat16 [4, 32, 48, 1536], P('dp', 'space', None, 'tensor')
- grad_input: bfloat16 [4, 32, 48, 1536], P('dp', 'space', None, 'tensor')
- grad_expand: float32 [1536, 6144], P(None, 'tensor')
- grad_project: float32 [6144, 1536], P('tensor')
- grad_kernel: float32 [7, 7, 1536], P(None, None, 'tensor')
The draws below stay inside these ranges and needn't reach their ends.
All inputs are finite; a program needn't handle non-finite values.
Results may differ from the reference program's by a relative error of at most 0.0067.
Values may be sent and summed in bfloat16 or wider, within the bound.
A program may use at most 192 MiB of HBM per device.

```python
import math
import jax
import jax.numpy as jnp
from jax import lax

C = 1536
FF = 6144
COLS = 48
IMAGES = 4
HEIGHT = 32


def draw_feature_map(key, part):
    scale_key, value_key = jax.random.split(key, 2)
    pixel_scale = jnp.exp(jax.random.uniform(scale_key, (IMAGES, HEIGHT, COLS, 1), jnp.float32, jnp.log(0.3), jnp.log(3.0)))
    values = jax.random.truncated_normal(value_key, -4.0, 4.0, (IMAGES, HEIGHT, COLS, C), jnp.float32)
    return (values * pixel_scale).astype(jnp.bfloat16)


def draw_conv_kernel(key, part):
    scale_key, value_key = jax.random.split(key, 2)
    ramp = jnp.exp(jnp.log(3.0) * jnp.arange(C, dtype=jnp.float32) / (C - 1))
    channel_scale = ramp * jnp.exp(jax.random.uniform(scale_key, (C,), jnp.float32, 0.0, jnp.log(3.3)))
    values = jax.random.truncated_normal(value_key, -4.0, 4.0, (7, 7, C), jnp.float32)
    return values * channel_scale / 7.0


def with_spikes(drawn, stream_key, source, target, blocks, factor):
    def block_of(dim):
        return (jnp.arange(drawn.shape[dim]) // (drawn.shape[dim] // blocks)).reshape((-1,) + (1,) * (drawn.ndim - 1 - dim))

    near = jax.random.permutation(stream_key, blocks)[block_of(target)]
    far = (block_of(target) + blocks // 2) % blocks
    return jnp.where((block_of(source) == near) | (block_of(source) == far), factor * drawn, drawn)


def steps_of(stream_key, shape, cuts, least, largest):
    def one(dim, parts):
        steps = jax.random.uniform(jax.random.fold_in(jax.random.fold_in(stream_key, 6), dim), (parts,), jnp.float32, least / len(cuts), largest / len(cuts))
        return jnp.repeat(jnp.exp(steps), shape[dim] // parts).reshape((-1,) + (1,) * (len(shape) - dim - 1))

    level = one(*cuts[0])
    for cut in cuts[1:]:
        level = level * one(*cut)
    return level


def scatter_about(stream_key, dims, spread, limit, cuts=(), kind=jnp.bfloat16):
    result = spread * jax.random.normal(stream_key, dims, jnp.float32)
    if cuts:
        result = result * steps_of(stream_key, dims, cuts, -0.22, 0.18)
    return jnp.clip(result, -limit, limit).astype(kind)


def noise_with(key, shape, spread, bound, cuts, heavy, kind=jnp.bfloat16):
    values = spread * jax.random.normal(key, shape, jnp.float32)
    if cuts:
        values = values * steps_of(key, shape, cuts, -0.22, 0.18)
    return jnp.clip(with_spikes(values, jax.random.fold_in(key, 3), *heavy), -bound, bound).astype(kind)


def setup_inputs(seed: int = 0) -> dict:
    key_list = jax.random.split(jax.random.key(seed), 12)
    return {
        "feature_map": draw_feature_map(jax.random.fold_in(key_list[11], 71), 0),
        "conv_kernel": draw_conv_kernel(jax.random.fold_in(key_list[11], 71), 0),
        "conv_bias": scatter_about(key_list[2], (C,), 1.0, 4.0, (), jnp.float32),
        "norm_gain": jnp.clip(1.0 + 0.18 * jax.random.normal(key_list[3], (C,), jnp.float32), 0.1, 1.9),
        "norm_bias": scatter_about(key_list[4], (C,), 0.5, 3.0, (), jnp.float32),
        "expand_weight": noise_with(key_list[5], (C, FF), C ** -0.5, 0.21875, ((1, 2),), (1, 0, 2, 2.0)),
        "expand_bias": scatter_about(key_list[6], (FF,), 0.5, 3.0, ((0, 2),), jnp.float32),
        "project_weight": noise_with(key_list[7], (FF, C), FF ** -0.5, 0.109375, ((0, 2),), (0, 1, 2, 2.0)),
        "project_bias": scatter_about(key_list[8], (C,), 0.5, 3.0, ((0, 2),), jnp.float32),
        "layer_scale": jnp.clip(jnp.exp(math.log(1.5) - 1.60943787 * jax.random.uniform(key_list[9], (C,), jnp.float32) ** steps_of(key_list[9], (C,), ((0, 2),), -0.2, 0.2)), 0.3, 1.5),
        "cotangent": scatter_about(key_list[10], (IMAGES, HEIGHT, COLS, C), 1.0, 6.0, ((0, 4), (1, 4), (3, 2))),
    }


EPSILON = 1e-06
INV_ROOT_TWO = 0.7071067811865476
INV_ROOT_TAU = 0.3989422804014327

def depthwise(padded, tap_weights, row_count, col_count):
    widened = jnp.pad(padded, ((0, 0), (0, 0), (3, 3), (0, 0)))
    running = jnp.zeros((widened.shape[0], row_count, col_count, widened.shape[3]), jnp.float32)
    for tap_row in range(7):
        for tap_col in range(7):
            running = running + tap_weights[tap_row, tap_col] * widened[:, tap_row:tap_row + row_count, tap_col:tap_col + col_count, :]
    return running

def kernel_grad(grad_float, padded, row_count, col_count):
    widened = jnp.pad(padded, ((0, 0), (0, 0), (3, 3), (0, 0)))
    tap_rows = []
    for tap_row in range(7):
        tap_line = []
        for tap_col in range(7):
            window = widened[:, tap_row:tap_row + row_count, tap_col:tap_col + col_count, :]
            tap_line.append(lax.optimization_barrier(jnp.sum(grad_float * window, axis=(0, 1, 2))))
        tap_rows.append(jnp.stack(tap_line))
    return jnp.stack(tap_rows)

def gelu_slope(values):
    cumulative = 0.5 * (1.0 + lax.erf(values * INV_ROOT_TWO))
    density = jnp.exp(-0.5 * values * values) * INV_ROOT_TAU
    return cumulative + values * density

def reference(feature_map, conv_kernel, conv_bias, norm_gain, norm_bias, expand_weight, expand_bias, project_weight, project_bias, layer_scale, cotangent):
    row_count = feature_map.shape[1]
    col_count = feature_map.shape[2]
    source = feature_map.astype(jnp.float32)
    padded = jnp.pad(source, ((0, 0), (3, 3), (0, 0), (0, 0)))
    filtered = depthwise(padded, conv_kernel, row_count, col_count) + conv_bias
    average = lax.optimization_barrier(jnp.mean(filtered, axis=-1, keepdims=True))
    centered = filtered - average
    inverse = lax.rsqrt(lax.optimization_barrier(jnp.mean(centered * centered, axis=-1, keepdims=True)) + EPSILON)
    unit_norm = (centered * inverse).reshape(-1, C)
    inverse = inverse.reshape(-1, 1)
    normed = (unit_norm * norm_gain + norm_bias).astype(jnp.bfloat16)
    hidden = jnp.dot(normed, expand_weight, preferred_element_type=jnp.float32) + expand_bias
    activated = jax.nn.gelu(hidden, approximate=False).astype(jnp.bfloat16)
    projected = jnp.dot(activated, project_weight, preferred_element_type=jnp.float32)
    block_out = (source.reshape(-1, C) + layer_scale * (projected + project_bias)).astype(jnp.bfloat16).reshape(feature_map.shape)
    grad_scaled = (cotangent.reshape(-1, C).astype(jnp.float32) * layer_scale).astype(jnp.bfloat16)
    grad_project = jnp.dot(activated.T, grad_scaled, preferred_element_type=jnp.float32)
    grad_act = jnp.dot(grad_scaled, project_weight.T, preferred_element_type=jnp.float32)
    grad_hidden = (grad_act * gelu_slope(hidden)).astype(jnp.bfloat16)
    grad_expand = jnp.dot(normed.T, grad_hidden, preferred_element_type=jnp.float32)
    grad_normed = jnp.dot(grad_hidden, expand_weight.T, preferred_element_type=jnp.float32)
    scaled_grad = grad_normed * norm_gain
    first_mean = lax.optimization_barrier(jnp.mean(scaled_grad, axis=1, keepdims=True))
    second_mean = lax.optimization_barrier(jnp.mean(scaled_grad * unit_norm, axis=1, keepdims=True))
    grad_filtered = ((scaled_grad - first_mean - unit_norm * second_mean) * inverse).astype(jnp.bfloat16)
    grad_float = grad_filtered.astype(jnp.float32).reshape(feature_map.shape)
    grad_kernel = kernel_grad(grad_float, padded, row_count, col_count)
    grad_padded = jnp.pad(grad_float, ((0, 0), (3, 3), (0, 0), (0, 0)))
    grad_input = (cotangent.astype(jnp.float32) + depthwise(grad_padded, conv_kernel[::-1, ::-1], row_count, col_count)).astype(jnp.bfloat16)
    return (block_out, grad_input, grad_expand, grad_project, grad_kernel)
```

```python
import jax
import jax.numpy as jnp
from jax import lax
from jax.sharding import PartitionSpec as P

EPSILON = 1e-06
INV_ROOT_TWO = 0.7071067811865476
INV_ROOT_TAU = 0.3989422804014327


def padded_2(block, sides, width):
    for axis, dim in sides:
        count = lax.axis_size(axis)
        forward = [(i, i + 1) for i in range(count - 1)]
        backward = [(target, source) for source, target in forward]
        low = lax.ppermute(
            lax.slice_in_dim(block, block.shape[dim] - width, None, axis=dim), axis, forward
        )
        high = lax.ppermute(lax.slice_in_dim(block, 0, width, axis=dim), axis, backward)
        block = jnp.concatenate([low, block, high], axis=dim)
    return block


def row_rims(block_data):
    return padded_2(block_data, (("space", 1),), 3)


def all_channels(block_data):
    return lax.all_gather(block_data, "tensor", axis=1, tiled=True)


def channel_total(stacked):
    return lax.psum(stacked, "tensor")


def partial_sums(term_rows):
    return lax.psum_scatter(term_rows, "tensor", scatter_dimension=1, tiled=True)


def pixel_total(term, dim):
    shared = lax.psum_scatter(term, ("dp", "space"), scatter_dimension=dim, tiled=True)
    whole = lax.all_gather(shared.astype(jnp.bfloat16), ("dp", "space"), axis=dim, tiled=True)
    return whole.astype(jnp.float32)


def depthwise(padded, tap_weights, row_count, col_count):
    widened = jnp.pad(padded.astype(jnp.float32), ((0, 0), (0, 0), (3, 3), (0, 0)))
    running = jnp.zeros((widened.shape[0], row_count, col_count, widened.shape[3]), jnp.float32)
    for tap_row in range(7):
        for tap_col in range(7):
            running = (
                running
                + tap_weights[tap_row, tap_col]
                * widened[:, tap_row : tap_row + row_count, tap_col : tap_col + col_count, :]
            )
    return running


def kernel_grad(grad_block, padded, row_count, col_count):
    widened = jnp.pad(padded.astype(jnp.float32), ((0, 0), (0, 0), (3, 3), (0, 0)))
    grad_float = grad_block.astype(jnp.float32)
    tap_rows = []
    for tap_row in range(7):
        tap_line = []
        for tap_col in range(7):
            window = widened[:, tap_row : tap_row + row_count, tap_col : tap_col + col_count, :]
            tap_line.append(jnp.sum(grad_float * window, axis=(0, 1, 2)))
        tap_rows.append(jnp.stack(tap_line))
    return jnp.stack(tap_rows)


def gelu_slope(values):
    cumulative = 0.5 * (1.0 + lax.erf(values * INV_ROOT_TWO))
    density = jnp.exp(-0.5 * values * values) * INV_ROOT_TAU
    return cumulative + values * density


def body(
    feature_map,
    conv_kernel,
    conv_bias,
    norm_gain,
    norm_bias,
    expand_weight,
    expand_bias,
    project_weight,
    project_bias,
    layer_scale,
    cotangent,
):
    images, row_count, col_count, shard_width = feature_map.shape
    pixels = images * row_count * col_count
    full_width = expand_weight.shape[0]
    offset = lax.axis_index("tensor") * shard_width
    own_gain = lax.dynamic_slice_in_dim(norm_gain, offset, shard_width, 0)
    own_kernel = lax.dynamic_slice_in_dim(conv_kernel, offset, shard_width, 2)
    padded = row_rims(feature_map)
    own_bias = lax.dynamic_slice_in_dim(conv_bias, offset, shard_width, 0)
    own_shift = lax.dynamic_slice_in_dim(norm_bias, offset, shard_width, 0)
    filtered = (depthwise(padded, own_kernel, row_count, col_count) + own_bias).reshape(
        pixels, shard_width
    )
    average = channel_total(jnp.sum(filtered, axis=1)) / full_width
    centered = filtered - average[:, None]
    spread = channel_total(jnp.sum(centered * centered, axis=1)) / full_width
    inverse = lax.rsqrt(spread + EPSILON)[:, None]
    unit_norm = centered * inverse
    gathered = all_channels((unit_norm * own_gain + own_shift).astype(jnp.bfloat16))
    hidden = jnp.dot(gathered, expand_weight, preferred_element_type=jnp.float32) + expand_bias
    activated = jax.nn.gelu(hidden, approximate=False).astype(jnp.bfloat16)
    projected = partial_sums(jnp.dot(activated, project_weight, preferred_element_type=jnp.float32))
    residual = feature_map.reshape(pixels, shard_width).astype(jnp.float32)
    block_out = (
        (residual + layer_scale * (projected + project_bias))
        .astype(jnp.bfloat16)
        .reshape(feature_map.shape)
    )
    grad_scaled = (cotangent.reshape(pixels, shard_width).astype(jnp.float32) * layer_scale).astype(
        jnp.bfloat16
    )
    grad_full = all_channels(grad_scaled)
    grad_project = pixel_total(
        lax.dot_general(
            activated, grad_full, (((0,), (0,)), ((), ())), preferred_element_type=jnp.float32
        ),
        1,
    )
    grad_act = lax.dot_general(
        grad_full, project_weight, (((1,), (1,)), ((), ())), preferred_element_type=jnp.float32
    )
    grad_hidden = (grad_act * gelu_slope(hidden)).astype(jnp.bfloat16)
    grad_expand = pixel_total(
        lax.dot_general(
            gathered, grad_hidden, (((0,), (0,)), ((), ())), preferred_element_type=jnp.float32
        ),
        0,
    )
    normed_terms = lax.dot_general(
        grad_hidden, expand_weight, (((1,), (1,)), ((), ())), preferred_element_type=jnp.float32
    )
    grad_normed = partial_sums(normed_terms)
    scaled_grad = grad_normed * own_gain
    channel_means = (
        lax.psum(
            jnp.stack([jnp.sum(scaled_grad, axis=1), jnp.sum(scaled_grad * unit_norm, axis=1)]),
            "tensor",
        )
        / full_width
    )
    grad_filtered = (
        (scaled_grad - channel_means[0][:, None] - unit_norm * channel_means[1][:, None]) * inverse
    ).astype(jnp.bfloat16)
    grad_block = grad_filtered.reshape(images, row_count, col_count, shard_width)
    grad_kernel = kernel_grad(grad_block, padded, row_count, col_count)
    grad_padded = row_rims(grad_block)
    grad_input = (
        cotangent.astype(jnp.float32)
        + depthwise(grad_padded, own_kernel[::-1, ::-1], row_count, col_count)
    ).astype(jnp.bfloat16)
    grad_kernel = lax.psum(grad_kernel, ("dp", "space"))
    return (block_out, grad_input, grad_expand, grad_project, grad_kernel)


def solution(mesh):
    in_specs = (
        P("dp", "space", None, "tensor"),
        P(),
        P(),
        P(),
        P(),
        P(None, "tensor"),
        P("tensor"),
        P("tensor", None),
        P("tensor"),
        P("tensor"),
        P("dp", "space", None, "tensor"),
    )
    out_specs = (
        P("dp", "space", None, "tensor"),
        P("dp", "space", None, "tensor"),
        P(None, "tensor"),
        P("tensor", None),
        P(None, None, "tensor"),
    )
    return jax.shard_map(body, mesh=mesh, in_specs=in_specs, out_specs=out_specs, check_vma=False)
```

```python
import jax
import jax.numpy as jnp
from jax import lax
from jax.sharding import PartitionSpec as P

EPSILON = 1e-06
INV_ROOT_TWO = 0.7071067811865476
INV_ROOT_TAU = 0.3989422804014327


def padded_2(block, sides, width):
    for axis, dim in sides:
        count = lax.axis_size(axis)
        forward = [(i, i + 1) for i in range(count - 1)]
        backward = [(target, source) for source, target in forward]
        low = lax.ppermute(
            lax.slice_in_dim(block, block.shape[dim] - width, None, axis=dim), axis, forward
        )
        high = lax.ppermute(lax.slice_in_dim(block, 0, width, axis=dim), axis, backward)
        block = jnp.concatenate([low, block, high], axis=dim)
    return block


def row_rims(block_data):
    return padded_2(block_data, (("space", 1),), 3)


def all_channels(block_data):
    return lax.all_gather(block_data, "tensor", axis=1, tiled=True)


def channel_total(stacked):
    return lax.psum(stacked, "tensor")


def partial_sums(term_rows):
    return lax.psum_scatter(term_rows, "tensor", scatter_dimension=1, tiled=True)


def pixel_total(term, dim):
    shared = lax.psum_scatter(term, ("dp", "space"), scatter_dimension=dim, tiled=True)
    whole = lax.all_gather(shared.astype(jnp.bfloat16), ("dp", "space"), axis=dim, tiled=True)
    return whole.astype(jnp.float32)


def depthwise(padded, tap_weights, row_count, col_count):
    widened = jnp.pad(padded.astype(jnp.float32), ((0, 0), (0, 0), (3, 3), (0, 0)))
    running = jnp.zeros((widened.shape[0], row_count, col_count, widened.shape[3]), jnp.float32)
    for tap_row in range(7):
        for tap_col in range(7):
            running = (
                running
                + tap_weights[tap_row, tap_col]
                * widened[:, tap_row : tap_row + row_count, tap_col : tap_col + col_count, :]
            )
    return running


def kernel_grad(grad_block, padded, row_count, col_count):
    widened = jnp.pad(padded.astype(jnp.float32), ((0, 0), (0, 0), (3, 3), (0, 0)))
    grad_float = grad_block.astype(jnp.float32)
    tap_rows = []
    for tap_row in range(7):
        tap_line = []
        for tap_col in range(7):
            window = widened[:, tap_row : tap_row + row_count, tap_col : tap_col + col_count, :]
            tap_line.append(jnp.sum(grad_float * window, axis=(0, 1, 2)))
        tap_rows.append(jnp.stack(tap_line))
    return jnp.stack(tap_rows)


def gelu_slope(values):
    cumulative = 0.5 * (1.0 + lax.erf(values * INV_ROOT_TWO))
    density = jnp.exp(-0.5 * values * values) * INV_ROOT_TAU
    return cumulative + values * density


def body(
    feature_map,
    conv_kernel,
    conv_bias,
    norm_gain,
    norm_bias,
    expand_weight,
    expand_bias,
    project_weight,
    project_bias,
    layer_scale,
    cotangent,
):
    images, row_count, col_count, shard_width = feature_map.shape
    pixels = images * row_count * col_count
    full_width = expand_weight.shape[0]
    offset = lax.axis_index("tensor") * shard_width
    own_gain = lax.dynamic_slice_in_dim(norm_gain, offset, shard_width, 0)
    own_kernel = lax.dynamic_slice_in_dim(conv_kernel, offset, shard_width, 2)
    padded = row_rims(feature_map)
    own_bias = lax.dynamic_slice_in_dim(conv_bias, offset, shard_width, 0)
    own_shift = lax.dynamic_slice_in_dim(norm_bias, offset, shard_width, 0)
    filtered = (depthwise(padded, own_kernel, row_count, col_count) + own_bias).reshape(
        pixels, shard_width
    )
    average = channel_total(jnp.sum(filtered, axis=1)) / full_width
    centered = filtered - average[:, None]
    spread = channel_total(jnp.sum(centered * centered, axis=1)) / full_width
    inverse = lax.rsqrt(spread + EPSILON)[:, None]
    unit_norm = centered * inverse
    gathered = all_channels((unit_norm * own_gain + own_shift).astype(jnp.bfloat16))
    hidden = jnp.dot(gathered, expand_weight, preferred_element_type=jnp.float32) + expand_bias
    activated = jax.nn.gelu(hidden, approximate=False).astype(jnp.bfloat16)
    projected = partial_sums(jnp.dot(activated, project_weight, preferred_element_type=jnp.float32))
    residual = feature_map.reshape(pixels, shard_width).astype(jnp.float32)
    block_out = (
        (residual + layer_scale * (projected + project_bias))
        .astype(jnp.bfloat16)
        .reshape(feature_map.shape)
    )
    grad_scaled = (cotangent.reshape(pixels, shard_width).astype(jnp.float32) * layer_scale).astype(
        jnp.bfloat16
    )
    grad_full = all_channels(grad_scaled)
    project_terms = lax.dot_general(
        activated, grad_full, (((0,), (0,)), ((), ())), preferred_element_type=jnp.float32
    )
    grad_act = lax.dot_general(
        grad_full, project_weight, (((1,), (1,)), ((), ())), preferred_element_type=jnp.float32
    )
    grad_hidden = (grad_act * gelu_slope(hidden)).astype(jnp.bfloat16)
    expand_terms = lax.dot_general(
        gathered, grad_hidden, (((0,), (0,)), ((), ())), preferred_element_type=jnp.float32
    )
    normed_terms = lax.dot_general(
        grad_hidden, expand_weight, (((1,), (1,)), ((), ())), preferred_element_type=jnp.float32
    )
    grad_normed = partial_sums(normed_terms)
    grad_normed, project_terms, expand_terms = lax.optimization_barrier(
        (grad_normed, project_terms, expand_terms)
    )
    grad_project = pixel_total(project_terms, 1)
    scaled_grad = grad_normed * own_gain
    channel_means = (
        lax.psum(
            jnp.stack([jnp.sum(scaled_grad, axis=1), jnp.sum(scaled_grad * unit_norm, axis=1)]),
            "tensor",
        )
        / full_width
    )
    grad_filtered = (
        (scaled_grad - channel_means[0][:, None] - unit_norm * channel_means[1][:, None]) * inverse
    ).astype(jnp.bfloat16)
    grad_block = grad_filtered.reshape(images, row_count, col_count, shard_width)
    grad_kernel = kernel_grad(grad_block, padded, row_count, col_count)
    grad_padded = row_rims(grad_block)
    grad_input = (
        cotangent.astype(jnp.float32)
        + depthwise(grad_padded, own_kernel[::-1, ::-1], row_count, col_count)
    ).astype(jnp.bfloat16)
    kernel_flat = grad_kernel.reshape(-1)
    hidden_shard = expand_terms.shape[1]
    extra = -(-kernel_flat.size // hidden_shard)
    extra = -(-(full_width + extra) // 8) * 8 - full_width
    kernel_rows = jnp.pad(kernel_flat, (0, extra * hidden_shard - kernel_flat.size)).reshape(
        extra, hidden_shard
    )
    merged = pixel_total(jnp.concatenate([expand_terms, kernel_rows]), 1)
    grad_expand = merged[:full_width]
    grad_kernel = merged[full_width:].reshape(-1)[: kernel_flat.size].reshape(grad_kernel.shape)
    return (block_out, grad_input, grad_expand, grad_project, grad_kernel)


def solution(mesh):
    in_specs = (
        P("dp", "space", None, "tensor"),
        P(),
        P(),
        P(),
        P(),
        P(None, "tensor"),
        P("tensor"),
        P("tensor", None),
        P("tensor"),
        P("tensor"),
        P("dp", "space", None, "tensor"),
    )
    out_specs = (
        P("dp", "space", None, "tensor"),
        P("dp", "space", None, "tensor"),
        P(None, "tensor"),
        P("tensor", None),
        P(None, None, "tensor"),
    )
    return jax.shard_map(body, mesh=mesh, in_specs=in_specs, out_specs=out_specs, check_vma=False)
```

```python
import jax
import jax.numpy as jnp
from jax import lax
from jax.sharding import PartitionSpec as P

EPSILON = 1e-06
INV_ROOT_TWO = 0.7071067811865476
INV_ROOT_TAU = 0.3989422804014327


def padded_2(block, sides, width):
    for axis, dim in sides:
        count = lax.axis_size(axis)
        forward = [(i, i + 1) for i in range(count - 1)]
        backward = [(target, source) for source, target in forward]
        low = lax.ppermute(
            lax.slice_in_dim(block, block.shape[dim] - width, None, axis=dim), axis, forward
        )
        high = lax.ppermute(lax.slice_in_dim(block, 0, width, axis=dim), axis, backward)
        block = jnp.concatenate([low, block, high], axis=dim)
    return block


def row_rims(block_data):
    return padded_2(block_data, (("space", 1),), 3)


def all_channels(block_data):
    return lax.all_gather(block_data, "tensor", axis=1, tiled=True)


def channel_total(stacked):
    return lax.psum(stacked, "tensor")


def partial_sums(term_rows):
    return lax.psum_scatter(term_rows, "tensor", scatter_dimension=1, tiled=True)


def pixel_total(term, dim):
    shared = lax.psum_scatter(term, ("dp", "space"), scatter_dimension=dim, tiled=True)
    whole = lax.all_gather(shared.astype(jnp.bfloat16), ("dp", "space"), axis=dim, tiled=True)
    return whole.astype(jnp.float32)


def depthwise(padded, tap_weights, row_count, col_count):
    widened = jnp.pad(padded.astype(jnp.float32), ((0, 0), (0, 0), (3, 3), (0, 0)))
    running = jnp.zeros((widened.shape[0], row_count, col_count, widened.shape[3]), jnp.float32)
    for tap_row in range(7):
        for tap_col in range(7):
            running = (
                running
                + tap_weights[tap_row, tap_col]
                * widened[:, tap_row : tap_row + row_count, tap_col : tap_col + col_count, :]
            )
    return running


def kernel_grad(grad_block, padded, row_count, col_count):
    widened = jnp.pad(padded.astype(jnp.float32), ((0, 0), (0, 0), (3, 3), (0, 0)))
    grad_float = grad_block.astype(jnp.float32)
    tap_rows = []
    for tap_row in range(7):
        tap_line = []
        for tap_col in range(7):
            window = widened[:, tap_row : tap_row + row_count, tap_col : tap_col + col_count, :]
            tap_line.append(jnp.sum(grad_float * window, axis=(0, 1, 2)))
        tap_rows.append(jnp.stack(tap_line))
    return jnp.stack(tap_rows)


def gelu_slope(values):
    cumulative = 0.5 * (1.0 + lax.erf(values * INV_ROOT_TWO))
    density = jnp.exp(-0.5 * values * values) * INV_ROOT_TAU
    return cumulative + values * density


def body(
    feature_map,
    conv_kernel,
    conv_bias,
    norm_gain,
    norm_bias,
    expand_weight,
    expand_bias,
    project_weight,
    project_bias,
    layer_scale,
    cotangent,
):
    images, row_count, col_count, shard_width = feature_map.shape
    pixels = images * row_count * col_count
    full_width = expand_weight.shape[0]
    offset = lax.axis_index("tensor") * shard_width
    own_gain = lax.dynamic_slice_in_dim(norm_gain, offset, shard_width, 0)
    own_kernel = lax.dynamic_slice_in_dim(conv_kernel, offset, shard_width, 2)
    padded = row_rims(feature_map)
    own_bias = lax.dynamic_slice_in_dim(conv_bias, offset, shard_width, 0)
    own_shift = lax.dynamic_slice_in_dim(norm_bias, offset, shard_width, 0)
    filtered = (depthwise(padded, own_kernel, row_count, col_count) + own_bias).reshape(
        pixels, shard_width
    )
    average = channel_total(jnp.sum(filtered, axis=1)) / full_width
    centered = filtered - average[:, None]
    spread = channel_total(jnp.sum(centered * centered, axis=1)) / full_width
    inverse = lax.rsqrt(spread + EPSILON)[:, None]
    unit_norm = centered * inverse
    gathered = all_channels((unit_norm * own_gain + own_shift).astype(jnp.bfloat16))
    hidden = jnp.dot(gathered, expand_weight, preferred_element_type=jnp.float32) + expand_bias
    activated = jax.nn.gelu(hidden, approximate=False).astype(jnp.bfloat16)
    projected = partial_sums(jnp.dot(activated, project_weight, preferred_element_type=jnp.float32))
    residual = feature_map.reshape(pixels, shard_width).astype(jnp.float32)
    block_out = (
        (residual + layer_scale * (projected + project_bias))
        .astype(jnp.bfloat16)
        .reshape(feature_map.shape)
    )
    grad_scaled = (cotangent.reshape(pixels, shard_width).astype(jnp.float32) * layer_scale).astype(
        jnp.bfloat16
    )
    grad_full = all_channels(grad_scaled)
    project_terms = lax.dot_general(
        activated, grad_full, (((0,), (0,)), ((), ())), preferred_element_type=jnp.float32
    )
    grad_act = lax.dot_general(
        grad_full, project_weight, (((1,), (1,)), ((), ())), preferred_element_type=jnp.float32
    )
    grad_hidden = (grad_act * gelu_slope(hidden)).astype(jnp.bfloat16)
    expand_terms = lax.dot_general(
        gathered, grad_hidden, (((0,), (0,)), ((), ())), preferred_element_type=jnp.float32
    )
    normed_terms = lax.dot_general(
        grad_hidden, expand_weight, (((1,), (1,)), ((), ())), preferred_element_type=jnp.float32
    )
    grad_normed = partial_sums(normed_terms)
    grad_normed, project_terms, expand_terms = lax.optimization_barrier(
        (grad_normed, project_terms, expand_terms)
    )
    grad_project = pixel_total(project_terms, 0)
    scaled_grad = grad_normed * own_gain
    channel_means = (
        lax.psum(
            jnp.stack([jnp.sum(scaled_grad, axis=1), jnp.sum(scaled_grad * unit_norm, axis=1)]),
            "tensor",
        )
        / full_width
    )
    grad_filtered = (
        (scaled_grad - channel_means[0][:, None] - unit_norm * channel_means[1][:, None]) * inverse
    ).astype(jnp.bfloat16)
    grad_block = grad_filtered.reshape(images, row_count, col_count, shard_width)
    grad_kernel = kernel_grad(grad_block, padded, row_count, col_count)
    grad_padded = row_rims(grad_block)
    grad_input = (
        cotangent.astype(jnp.float32)
        + depthwise(grad_padded, own_kernel[::-1, ::-1], row_count, col_count)
    ).astype(jnp.bfloat16)
    kernel_flat = grad_kernel.reshape(-1)
    hidden_shard = expand_terms.shape[1]
    extra = -(-kernel_flat.size // hidden_shard)
    extra = -(-(full_width + extra) // 8) * 8 - full_width
    kernel_rows = jnp.pad(kernel_flat, (0, extra * hidden_shard - kernel_flat.size)).reshape(
        extra, hidden_shard
    )
    merged = pixel_total(jnp.concatenate([expand_terms, kernel_rows]), 1)
    grad_expand = merged[:full_width]
    grad_kernel = merged[full_width:].reshape(-1)[: kernel_flat.size].reshape(grad_kernel.shape)
    return (block_out, grad_input, grad_expand, grad_project, grad_kernel)


def solution(mesh):
    in_specs = (
        P("dp", "space", None, "tensor"),
        P(),
        P(),
        P(),
        P(),
        P(None, "tensor"),
        P("tensor"),
        P("tensor", None),
        P("tensor"),
        P("tensor"),
        P("dp", "space", None, "tensor"),
    )
    out_specs = (
        P("dp", "space", None, "tensor"),
        P("dp", "space", None, "tensor"),
        P(None, "tensor"),
        P("tensor", None),
        P(None, None, "tensor"),
    )
    return jax.shard_map(body, mesh=mesh, in_specs=in_specs, out_specs=out_specs, check_vma=False)
```
